32 devices in a mesh: acq: 4 (over z), line: 8 (over y, x, core).
Axes of the slice: x: 2, y: 2, z: 4, core: 2. Of those that a mesh axis runs over, the one named last changes fastest.
Arguments:
- slc_stack: float32 [2, 64, 64, 512], P(None, 'acq', 'line'), may hold values from -6 to 6
- wavenumbers: float32 [64], replicated, may hold values from -0.8 to 0.8
Outputs:
- spectrum: bfloat16 [256, 64, 512], P(None, 'line', 'acq')
The draws below stay inside these ranges and needn't reach their ends.
All inputs are finite; a program needn't handle non-finite values.
Results may differ from the reference program's by a relative error of at most 0.001.
Values sent between devices are 32-bit elements; how exact they have to be, the bound alone decides.
A program may use at most 64 MiB of HBM per device.

```python
import jax
import jax.numpy as jnp
from jax import lax

ACQS = 64
HEIGHTS = 256
LINE_DEV = 8
LINES = 64
RANGE = 512
N_LINE = 8


def block_scale(key, dims, pieces, smallest, largest):
    gain = 1.0
    for position, parts in pieces:
        steps = jax.random.uniform(jax.random.fold_in(jax.random.fold_in(key, 6), position), (parts,), jnp.float32, smallest / len(pieces), largest / len(pieces))
        gain = gain * jnp.repeat(jnp.exp(steps), dims[position] // parts).reshape((-1,) + (1,) * (len(dims) - 1 - position))
    return gain


def noise(own_key, shape, width, most, cuts=(), held_as=jnp.bfloat16):
    array = width * jax.random.normal(own_key, shape, jnp.float32)
    if cuts:
        array = array * block_scale(own_key, shape, cuts, -0.22, 0.18)
    return jnp.clip(array, -most, most).astype(held_as)


def setup_inputs(seed: int = 0) -> dict:
    streams_of = jax.random.split(jax.random.key(seed), 3)
    slc_stack = noise(streams_of[0], (2, ACQS, LINES, RANGE), 1.0, 6.0, ((1, 4), (2, 8)), jnp.float32)
    wavenumbers = jnp.clip(jax.random.uniform(streams_of[1], (ACQS,), jnp.float32, -0.8, 0.8), -0.8, 0.8)
    return dict(slc_stack=slc_stack, wavenumbers=wavenumbers)


epsilon = 1e-6


def steering(wavenumbers, count):
    heights = jnp.arange(count, dtype=jnp.int32).astype(jnp.float32) - jnp.float32(count // 2)
    phases = wavenumbers[:, None] * heights[None, :]
    cosine_part = jnp.cos(phases).T
    sine_part = jnp.sin(phases).T
    upper = jnp.concatenate([cosine_part, sine_part], axis=1)
    lower = jnp.concatenate([-sine_part, cosine_part], axis=1)
    return jnp.concatenate([upper, lower], axis=0)


def beamform(stack_block, wavenumbers, count):
    matrix = steering(wavenumbers, count)
    channels = stack_block.shape[0] * stack_block.shape[1]
    flat = stack_block.reshape(channels, -1)
    beams = jnp.dot(matrix, flat, precision=lax.Precision.HIGHEST, preferred_element_type=jnp.float32)
    beam_power = beams[:count] * beams[:count] + beams[count:] * beams[count:]
    energy = jnp.sum(flat * flat, axis=0)
    shape = stack_block.shape[2:]
    return beam_power.reshape((count,) + shape), energy.reshape((1,) + shape)


def sum_range(field, count):
    total = field[..., 0:count]
    for offset in range(1, 7):
        total = total + field[..., offset:offset + count]
    return total


def sum_lines(field, count):
    total = field[..., 0:count, :]
    for offset in range(1, 7):
        total = total + field[..., offset:offset + count, :]
    return total


def reference(slc_stack, wavenumbers):
    padded = jnp.pad(slc_stack, ((0, 0), (0, 0), (3, 3), (3, 3)))
    range_count = slc_stack.shape[3]

    def one_block(block_index):
        first_line = (block_index * LINE_DEV).astype(jnp.int32)
        stack_block = lax.dynamic_slice_in_dim(padded, first_line, LINE_DEV + 6, 2)
        beam_power, energy = beamform(stack_block, wavenumbers, HEIGHTS)
        box_power = sum_lines(sum_range(beam_power, range_count), LINE_DEV)
        box_energy = sum_lines(sum_range(energy, range_count), LINE_DEV)
        return (box_power / (box_energy + epsilon)).astype(jnp.bfloat16)

    blocks = lax.map(one_block, jnp.arange(N_LINE, dtype=jnp.int32))
    return blocks.transpose(1, 0, 2, 3).reshape(HEIGHTS, LINE_DEV * N_LINE, range_count)
```

```python
import jax
import jax.numpy as jnp
from jax import lax
from jax.sharding import PartitionSpec as P

HEIGHTS = 256


epsilon = 1e-06


def with_line_halo(x, width):
    size, length = (lax.axis_size("line"), x.shape[2])
    up = [(i, i + 1) for i in range(size - 1)]
    down = [(j, i) for i, j in up]
    before = lax.ppermute(x[:, :, length - width :], "line", up)
    after = lax.ppermute(x[:, :, :width], "line", down)
    return jnp.concatenate([before, x, after], axis=2)


def range_halo(x, width):
    parts, acqs, lines, cells = x.shape
    size = lax.axis_size("acq")
    block = cells // size
    padded = jnp.pad(x, ((0, 0), (0, 0), (0, 0), (width, width)))
    edges = []
    for d in range(size):
        left = padded[..., d * block : d * block + width]
        start = (d + 1) * block + width
        right = padded[..., start : start + width]
        edges.append(jnp.concatenate([left, right], axis=3))
    sent = jnp.stack(edges).reshape(size, parts * acqs, lines * 2 * width)
    got = lax.all_to_all(sent, "acq", split_axis=0, concat_axis=0, tiled=True)
    got = got.reshape(size, parts, acqs, lines, 2 * width).transpose(1, 0, 2, 3, 4)
    return got.reshape(parts, size * acqs, lines, 2 * width)


def steering(wavenumbers, count):
    heights = jnp.arange(count, dtype=jnp.int32).astype(jnp.float32) - jnp.float32(count // 2)
    phases = wavenumbers[:, None] * heights[None, :]
    cosine_part = jnp.cos(phases).T
    sine_part = jnp.sin(phases).T
    upper = jnp.concatenate([cosine_part, sine_part], axis=1)
    lower = jnp.concatenate([-sine_part, cosine_part], axis=1)
    return jnp.concatenate([upper, lower], axis=0)


def beamform(stack_block, matrix, count):
    channels = stack_block.shape[0] * stack_block.shape[1]
    flat = stack_block.reshape(channels, -1)
    beams = jnp.dot(
        matrix, flat, precision=lax.Precision.HIGH, preferred_element_type=jnp.float32
    )
    beam_power = beams[:count] * beams[:count] + beams[count:] * beams[count:]
    energy = jnp.sum(flat * flat, axis=0)
    shape = stack_block.shape[2:]
    return (beam_power.reshape((count,) + shape), energy.reshape((1,) + shape))


def sum_range(field, count):
    total = field[..., 0:count]
    for offset in range(1, 7):
        total = total + field[..., offset : offset + count]
    return total


def sum_lines(field, count):
    total = field[..., 0:count, :]
    for offset in range(1, 7):
        total = total + field[..., offset : offset + count, :]
    return total


def body(slc_stack, wavenumbers):
    width = 3
    line_count = slc_stack.shape[2]
    tall = with_line_halo(slc_stack, width)
    edge = range_halo(tall, width)
    regrouped = lax.all_to_all(tall, "acq", split_axis=3, concat_axis=1, tiled=True)
    range_count = regrouped.shape[3]
    matrix = steering(wavenumbers, HEIGHTS)
    inner = beamform(regrouped, matrix, HEIGHTS)
    outer = beamform(edge, matrix, HEIGHTS)
    boxes = []
    for mid, rim in zip(inner, outer):
        mid, rim = (sum_lines(mid, line_count), sum_lines(rim, line_count))
        wide = jnp.concatenate([rim[..., :width], mid, rim[..., width:]], axis=-1)
        boxes.append(sum_range(wide, range_count))
    return (boxes[0] / (boxes[1] + epsilon)).astype(jnp.bfloat16)


def solution(mesh):
    placed = (P(None, "acq", "line", None), P())
    return jax.shard_map(
        body, mesh=mesh, in_specs=placed, out_specs=P(None, "line", "acq"), check_vma=False
    )
```
